512 devices in a mesh: row: 16 (over y, x), col: 32 (over z, core).
Axes of the slice: x: 4, y: 4, z: 16, core: 2. Of those that a mesh axis runs over, the one named last changes fastest.
Arguments:
- panel: bfloat16 [4, 16, 512, 512], P(None, 'row', 'col'), may hold values from -1.1953125 to 1.1953125
- inverse_factor: bfloat16 [512, 512], replicated
- slot_rows: int32 [16, 32, 2], P('row', 'col'), may hold values from 0 to 63, as said below
- slot_cols: int32 [16, 32, 2], P('row', 'col'), may hold values from 0 to 63, as said below
- live_count: int32 [16, 32], P('row', 'col'), may hold values from 0 to 2
Outputs:
- contrib: bfloat16 [16, 32, 2, 512, 512], P('row', 'col')
The draws below stay inside these ranges and needn't reach their ends.
Inputs may be any that keep to these rules, and one draw needn't show every extreme that they name: slot_rows[r, c, s] is congruent to r modulo 16; for s < live_count[r, c] the slots of one position name distinct blocks with slot_rows >= slot_cols; the other slots are ignored. slot_cols[r, c, s] is congruent to c modulo 32.
All inputs are finite; a program needn't handle non-finite values.
Results may differ from the reference program's by a relative error of at most 0.0054.
Values may be sent and summed in bfloat16 or wider, within the bound.
No kernel may reach another device: no remote copies, remote signals or barrier semaphores. Data moves between devices by JAX's collectives and lax.ppermute only.
A program may use at most 64 MiB of HBM per device.

```python
import jax
import jax.numpy as jnp
from jax import lax

B = 512
PR = 4
SLOTS = 2
N_ROW = 16
N_COL = 32


def slot_plan(key):
    col_ratio = N_COL // N_ROW
    per_row = PR // col_ratio
    count = PR * per_row
    candidate = jnp.arange(count, dtype=jnp.int32)
    cand_a = candidate // per_row
    cand_b = candidate % per_row
    row_index = jnp.arange(N_ROW, dtype=jnp.int32)[:, None, None]
    col_index = jnp.arange(N_COL, dtype=jnp.int32)[None, :, None]
    valid = row_index + N_ROW * cand_a >= col_index + N_COL * cand_b
    scores = jax.random.randint(jax.random.fold_in(key, 11), (N_ROW, N_COL, count), 0, 4096) * count + candidate
    scores = scores + jnp.where(valid, 0, 1 << 24)
    first_corner = (row_index == 0) & (col_index == 0) & (candidate[None, None, :] == 0)
    last_corner = (row_index == N_ROW - 1) & (col_index == N_COL - 1) & (candidate[None, None, :] == count - 1)
    scores = scores - jnp.where(first_corner | last_corner, 1 << 25, 0)
    order = jnp.argsort(scores, axis=-1)[..., :SLOTS].astype(jnp.int32)
    chosen_valid = jnp.take_along_axis(valid, order, axis=-1)
    pick_a = jnp.where(chosen_valid, order // per_row, 0)
    pick_b = jnp.where(chosen_valid, order % per_row, 0)
    rows_out = (row_index + N_ROW * pick_a).astype(jnp.int32)
    cols_out = (col_index + N_COL * pick_b).astype(jnp.int32)
    valid_count = jnp.sum(valid.astype(jnp.int32), axis=-1)
    wanted = jax.random.randint(jax.random.fold_in(key, 12), (N_ROW, N_COL), 1, SLOTS + 1)
    full_row = jax.random.randint(jax.random.fold_in(key, 13), (), 0, N_ROW)
    full_col = jax.random.randint(jax.random.fold_in(key, 14), (), 0, full_row + 1)
    forced = (jnp.arange(N_ROW)[:, None] == full_row) & (jnp.arange(N_COL)[None, :] == full_col)
    wanted = jnp.where(forced, SLOTS, wanted)
    live = jnp.minimum(valid_count, wanted).astype(jnp.int32)
    return (rows_out, cols_out, live)


def draw_slot_rows(key, part):
    return slot_plan(key)[0]


def draw_slot_cols(key, part):
    return slot_plan(key)[1]


def draw_live_count(key, part):
    return slot_plan(key)[2]


def draw_inverse_factor(key, part):
    diagonal = jnp.exp(jax.random.uniform(jax.random.fold_in(key, 21), (B,), minval=-0.7, maxval=0.7))
    upper_part = 0.035 * jax.random.normal(jax.random.fold_in(key, 22), (B, B))
    matrix = jnp.triu(upper_part, 1) + jnp.diag(diagonal)
    return matrix.astype(jnp.float32).astype(jnp.bfloat16)


def shard_levels(stream_key, shape, shards, low, high):
    gain, own = 1.0, jax.random.fold_in(stream_key, 6)
    for dim, parts in shards:
        steps = jnp.exp(jax.random.uniform(jax.random.fold_in(own, dim), (parts,), jnp.float32, low / len(shards), high / len(shards)))
        gain = gain * jnp.repeat(steps, shape[dim] // parts).reshape([-1 if axis == dim else 1 for axis in range(len(shape))])
    return gain


def normal_values(rng, shape, deviation, limit, split=(), kind=jnp.bfloat16):
    array = deviation * jax.random.normal(rng, shape, jnp.float32)
    if split:
        array = array * shard_levels(rng, shape, split, -0.22, 0.18)
    return jnp.clip(array, -limit, limit).astype(kind)


def setup_inputs(seed: int = 0) -> dict:
    key_list = jax.random.split(jax.random.key(seed), 6)
    panel = normal_values(key_list[0], (PR, N_ROW, B, B), 0.2, 1.1953125, ((1, 16), (2, 32)))
    inverse_factor = draw_inverse_factor(jax.random.fold_in(key_list[5], 71), 0)
    slot_rows = draw_slot_rows(jax.random.fold_in(key_list[5], 71), 0)
    slot_cols = draw_slot_cols(jax.random.fold_in(key_list[5], 71), 0)
    live_count = draw_live_count(jax.random.fold_in(key_list[5], 71), 0)
    return {"panel": panel, "inverse_factor": inverse_factor, "slot_rows": slot_rows, "slot_cols": slot_cols, "live_count": live_count}


def reference(panel, inverse_factor, slot_rows, slot_cols, live_count):
    factor = jnp.dot(panel.reshape(-1, B), inverse_factor, preferred_element_type=jnp.float32)
    factor = factor.astype(jnp.bfloat16).reshape(PR * N_ROW, B, B)
    slot_index = jnp.arange(SLOTS, dtype=jnp.int32)
    live_mask = (slot_index[None, None, :] < live_count[:, :, None]).reshape(-1)
    flat_rows = slot_rows.reshape(-1).astype(jnp.int32)
    flat_cols = slot_cols.reshape(-1).astype(jnp.int32)

    def slot_tile(item):
        block_row, block_col, flag = item
        left_tile = lax.dynamic_index_in_dim(factor, block_row, 0, keepdims=False)
        right_tile = lax.dynamic_index_in_dim(factor, block_col, 0, keepdims=False)
        product = jnp.dot(left_tile, right_tile.T, preferred_element_type=jnp.float32)
        return jnp.where(flag, -product, jnp.zeros_like(product)).astype(jnp.bfloat16)

    tiles = lax.map(slot_tile, (flat_rows, flat_cols, live_mask))
    return tiles.reshape(N_ROW, N_COL, SLOTS, B, B)
```

```python
import functools

import jax
import jax.numpy as jnp
from jax import lax
from jax.experimental import pallas as pl
from jax.experimental.pallas import tpu as pltpu
from jax.sharding import PartitionSpec as P

STEPS = (
    ((4, (0,)), (-4, (0,)), (8, (0,))),
    ((1, (0, -4, 4, 8)), (-1, (0, -4, 4, 8)), (2, (0, 8)), (-2, (0, 8))),
)
CHIPS = 16


def norm(offset):
    return (offset + 7) % CHIPS - 7


def shift_z(value, shift):
    size = 2 * CHIPS
    return lax.ppermute(value, "col", [(i, (i + 2 * shift) % size) for i in range(size)])


def swap_core(value):
    return lax.ppermute(value, "col", [(i, i ^ 1) for i in range(2 * CHIPS)])


def gather_left(piece):
    have = {0: piece}
    groups = [((0,), piece[None])]
    out = []
    for number, step in enumerate(STEPS):
        fresh, names, parts = {}, [], []
        for shift, offsets in step:
            sent = jnp.stack([have[o] for o in offsets])
            got = shift_z(sent, shift)
            for index, o in enumerate(offsets):
                name = norm(o - shift)
                if name not in have and name not in fresh:
                    fresh[name] = got[index]
                    names.append(name)
                    parts.append(got[index])
        have.update(fresh)
        if number == 0:
            names, parts = [0] + names, [piece] + parts
        group = jnp.stack(parts)
        out.append((tuple(names), group, swap_core(group)))
    return out


def gather_right(piece):
    rows = lax.axis_size("row")
    col = lax.axis_index("col")
    pair = piece.reshape(2, 2, *piece.shape[1:])
    got = []
    for k in range(2):
        half = (col + k) % 2
        sent = lax.dynamic_index_in_dim(pair, half, 1, keepdims=False)
        perm = [
            (r * 32 + c, (c // 2) * 32 + r + rows * ((c + k) % 2))
            for r in range(rows)
            for c in range(32)
        ]
        got.append(lax.ppermute(sent, ("row", "col"), perm))
    high = col // rows == 1
    both = jnp.stack(
        [jnp.where(high, got[1], got[0]), jnp.where(high, got[0], got[1])]
    )
    spread = jnp.broadcast_to(both[None], (rows, *both.shape))
    return lax.all_to_all(spread, "row", 0, 0, tiled=True)


def kernel(names, rows_ref, cols_ref, live_ref, w_ref, right_ref, *refs):
    lefts, out_ref, a_ref, f_ref = refs[:-3], refs[-3], refs[-2], refs[-1]
    col = lax.axis_index("col")
    z = lax.div(col, 2)
    core = lax.rem(col, 2)
    live = live_ref[0, 0]
    w = w_ref[...]
    size = w.shape[0]
    dims = (((1,), (1,)), ((), ()))
    for b in range(2):
        block = right_ref[:, :, b].reshape(size, size)
        f_ref[b] = jnp.dot(block, w, preferred_element_type=jnp.float32).astype(jnp.bfloat16)
    for slot in range(2):

        @pl.when(slot < live)
        def _():
            a = rows_ref[0, 0, slot] // 16
            b = cols_ref[0, 0, slot] // 32
            for group, offsets in enumerate(names):
                for index, offset in enumerate(offsets):
                    origin = lax.rem(z + offset + CHIPS, CHIPS)
                    for other in range(2):
                        who = core if other == 0 else 1 - core
                        start = pl.multiple_of((2 * origin + who) * 16, 16)
                        a_ref[pl.ds(start, 16), :] = lefts[2 * group + other][index, a]
            left = jnp.dot(a_ref[...], w, preferred_element_type=jnp.float32).astype(jnp.bfloat16)
            product = lax.dot_general(left, f_ref[b], dims, preferred_element_type=jnp.float32)
            out_ref[slot] = (-product).astype(jnp.bfloat16)

        @pl.when(slot >= live)
        def _():
            out_ref[slot] = jnp.zeros_like(out_ref[slot])


def body(panel, inverse_factor, slot_rows, slot_cols, live_count):
    piece = panel[:, 0]
    size = inverse_factor.shape[0]
    right = gather_right(piece)
    groups = gather_left(piece)
    names = tuple(g[0] for g in groups)
    lefts = [array for g in groups for array in g[1:]]
    smem = pl.BlockSpec(memory_space=pltpu.SMEM)
    vmem = pl.BlockSpec(memory_space=pltpu.VMEM)
    out = pl.pallas_call(
        functools.partial(kernel, names),
        out_shape=jax.ShapeDtypeStruct((2, size, size), jnp.bfloat16),
        in_specs=[smem] * 3 + [vmem] * (2 + len(lefts)),
        out_specs=vmem,
        scratch_shapes=[
            pltpu.VMEM((size, size), jnp.bfloat16),
            pltpu.VMEM((2, size, size), jnp.bfloat16),
        ],
        compiler_params=pltpu.CompilerParams(vmem_limit_bytes=32 * 2**20),
    )(slot_rows, slot_cols, live_count, inverse_factor, right, *lefts)
    return out[None, None]


def solution(mesh):
    placed = (
        P(None, "row", "col", None),
        P(),
        P("row", "col", None),
        P("row", "col", None),
        P("row", "col"),
    )
    return jax.shard_map(
        body,
        mesh=mesh,
        in_specs=placed,
        out_specs=P("row", "col", None, None, None),
        check_vma=False,
    )
```

```python
import functools

import jax
import jax.numpy as jnp
from jax import lax
from jax.experimental import pallas as pl
from jax.experimental.pallas import tpu as pltpu
from jax.sharding import PartitionSpec as P

CHIPS = 16
COLS = 2 * CHIPS
ROWS = 16
SIDE = 4


def swap_core(value):
    return lax.ppermute(value, "col", [(i, i ^ 1) for i in range(COLS)])


def spread_z(value, hops):
    return lax.ppermute(
        value, "col", [(i, (i + (2 * hops if i % 2 == 0 else -2 * hops)) % COLS) for i in range(COLS)]
    )


def ring(delta, size):
    return min(delta % size, -delta % size)


def relay_steps():
    along = sorted(range(CHIPS), key=lambda d: -ring(d, CHIPS))
    across = sorted(range(ROWS), key=lambda s: ring(s // SIDE, SIDE) + ring(s % SIDE, SIDE))
    steps = dict(zip(along, across))
    return [(steps[d] // SIDE, steps[d] % SIDE) for d in range(CHIPS)]


def relay_row(row, step):
    return (row // SIDE + step[0]) % SIDE * SIDE + (row + step[1]) % SIDE


def scatter(value):
    steps = relay_steps()
    perm = []
    for r in range(ROWS):
        for c in range(COLS):
            target = r + ROWS * (c % 2)
            step = steps[(c // 2 - target // 2) % CHIPS]
            perm.append((r * COLS + c, relay_row(r, step) * COLS + target))
    return lax.ppermute(value, ("row", "col"), perm)


def update_kernel(plan, rows_ref, cols_ref, live_ref, w_ref, right_ref, *refs):
    lefts, (out_ref, a_ref, f_ref) = refs[:-3], refs[-3:]
    col = lax.axis_index("col")
    z = lax.div(col, 2)
    core = lax.rem(col, 2)
    high = lax.div(col, ROWS)
    root = lax.rem(col, ROWS)
    live = live_ref[0, 0]
    w = w_ref[...]
    dims = (((1,), (1,)), ((), ()))

    def place(origin, part, tile):
        start = pl.multiple_of((2 * lax.rem(origin + 2 * CHIPS, CHIPS) + part) * 16, 16)
        a_ref[pl.ds(start, 16), :] = tile

    for b in range(2):
        for delta, step in enumerate(relay_steps()):
            row = lax.rem(lax.div(root, SIDE) + step[0], SIDE) * SIDE + lax.rem(root + step[1], SIDE)
            for part in range(2):
                place(z + delta, lax.rem(high + part, 2), right_ref[row, part, b])
        f_ref[b] = jnp.dot(a_ref[...], w, preferred_element_type=jnp.float32).astype(jnp.bfloat16)
    for slot in range(2):

        @pl.when(slot < live)
        def _():
            a = rows_ref[0, 0, slot] // ROWS
            b = cols_ref[0, 0, slot] // COLS
            for which, first, hops, swapped in plan:
                way, base = (1 - 2 * core, 1 - core) if swapped else (2 * core - 1, core)
                for index, (hop, part) in enumerate(hops):
                    place(z + way * hop, lax.rem(base + part, 2), lefts[which][first + index, a])
            left = jnp.dot(a_ref[...], w, preferred_element_type=jnp.float32).astype(jnp.bfloat16)
            product = lax.dot_general(left, f_ref[b], dims, preferred_element_type=jnp.float32)
            out_ref[slot] = (-product).astype(jnp.bfloat16)

        @pl.when(slot >= live)
        def _():
            out_ref[slot] = jnp.zeros_like(out_ref[slot])


def pairs(*hops):
    return tuple((hop, part) for hop in hops for part in range(2))


def body(panel, inverse_factor, slot_rows, slot_cols, live_count):
    piece = panel[:, 0]
    size = inverse_factor.shape[0]
    core = lax.axis_index("col") % 2

    other = swap_core(piece)
    pair = jnp.stack([piece, other])
    g4 = spread_z(pair, 4)
    mine = jnp.stack(
        [
            lax.dynamic_index_in_dim(part.reshape(2, 2, *piece.shape[1:]), core, 1, keepdims=False)
            for part in (piece, other)
        ]
    )
    scattered, g4 = lax.optimization_barrier((scatter(mine), g4))
    fanned = jnp.broadcast_to(scattered[None], (ROWS, *scattered.shape))
    right = lax.all_to_all(fanned, "row", 0, 0, tiled=True)

    near = jnp.concatenate([pair, g4])
    g2 = spread_z(near, 2)
    g1a = spread_z(near, 1)
    g1b = spread_z(g2, 1)
    edge = spread_z(g2[2:], 2)
    early = jnp.concatenate([g4, g2, g1a])
    early2 = swap_core(early)
    g1b, edge, right, early2 = lax.optimization_barrier((g1b, edge, right, early2))
    lefts = [pair, early, g1b, edge, early2, swap_core(g1b)]
    hops = pairs(4, 2, 6, 1, 5)
    plan = (
        (0, 0, pairs(0), False),
        (1, 0, hops, False),
        (2, 0, pairs(3, 7), False),
        (3, 0, pairs(8), False),
        (4, 0, hops, True),
        (5, 0, pairs(3, 7), True),
    )

    smem = pl.BlockSpec(memory_space=pltpu.SMEM)
    vmem = pl.BlockSpec(memory_space=pltpu.VMEM)
    out = pl.pallas_call(
        functools.partial(update_kernel, plan),
        out_shape=jax.ShapeDtypeStruct((2, size, size), jnp.bfloat16),
        in_specs=[smem] * 3 + [vmem] * (2 + len(lefts)),
        out_specs=vmem,
        scratch_shapes=[
            pltpu.VMEM((size, size), jnp.bfloat16),
            pltpu.VMEM((2, size, size), jnp.bfloat16),
        ],
        compiler_params=pltpu.CompilerParams(vmem_limit_bytes=16 * 2**20),
    )(slot_rows, slot_cols, live_count, inverse_factor, right, *lefts)
    return out[None, None]


def solution(mesh):
    placed = (
        P(None, "row", "col", None),
        P(),
        P("row", "col", None),
        P("row", "col", None),
        P("row", "col"),
    )
    return jax.shard_map(
        body,
        mesh=mesh,
        in_specs=placed,
        out_specs=P("row", "col", None, None, None),
        check_vma=False,
    )
```

```python
import functools

import jax
import jax.numpy as jnp
from jax import lax
from jax.experimental import pallas as pl
from jax.experimental.pallas import tpu as pltpu
from jax.sharding import PartitionSpec as P

CHIPS = 16
COLS = 2 * CHIPS
ROWS = 16
SIDE = 4


def swap_core(value):
    return lax.ppermute(value, "col", [(i, i ^ 1) for i in range(COLS)])


def spread_z(value, hops):
    return lax.ppermute(
        value, "col", [(i, (i + (2 * hops if i % 2 == 0 else -2 * hops)) % COLS) for i in range(COLS)]
    )


def ring(delta, size):
    return min(delta % size, -delta % size)


def relay_steps():
    along = sorted(range(CHIPS), key=lambda d: -ring(d, CHIPS))
    across = sorted(range(ROWS), key=lambda s: ring(s // SIDE, SIDE) + ring(s % SIDE, SIDE))
    steps = dict(zip(along, across))
    return [(steps[d] // SIDE, steps[d] % SIDE) for d in range(CHIPS)]


def relay_row(row, step):
    return (row // SIDE + step[0]) % SIDE * SIDE + (row + step[1]) % SIDE


def scatter(value):
    steps = relay_steps()
    perm = []
    for r in range(ROWS):
        for c in range(COLS):
            target = r + ROWS * (c % 2)
            step = steps[(c // 2 - target // 2) % CHIPS]
            perm.append((r * COLS + c, relay_row(r, step) * COLS + target))
    return lax.ppermute(value, ("row", "col"), perm)


def origin_row(origin, part):
    return pl.multiple_of((2 * lax.rem(origin + 2 * CHIPS, CHIPS) + part) * 16, 16)


def solve(value, w):
    return jnp.dot(value, w, preferred_element_type=jnp.float32).astype(jnp.bfloat16)


def right_kernel(w_ref, right_ref, f_ref, block_ref):
    col = lax.axis_index("col")
    z = lax.div(col, 2)
    high = lax.div(col, ROWS)
    root = lax.rem(col, ROWS)
    w = w_ref[...]
    for b in range(2):
        for delta, step in enumerate(relay_steps()):
            row = lax.rem(lax.div(root, SIDE) + step[0], SIDE) * SIDE + lax.rem(root + step[1], SIDE)
            for part in range(2):
                start = origin_row(z + delta, lax.rem(high + part, 2))
                block_ref[pl.ds(start, 16), :] = right_ref[row, part, b]
        f_ref[b] = solve(block_ref[...], w)


def update_kernel(plan, rows_ref, cols_ref, live_ref, w_ref, f_ref, *refs):
    lefts, (out_ref, a_ref) = refs[:-2], refs[-2:]
    col = lax.axis_index("col")
    z = lax.div(col, 2)
    core = lax.rem(col, 2)
    live = live_ref[0, 0]
    dims = (((1,), (1,)), ((), ()))
    for slot in range(2):

        @pl.when(slot < live)
        def _():
            a = rows_ref[0, 0, slot] // ROWS
            b = cols_ref[0, 0, slot] // COLS
            for which, first, hops, swapped in plan:
                way, base = (1 - 2 * core, 1 - core) if swapped else (2 * core - 1, core)
                for index, (hop, part) in enumerate(hops):
                    start = origin_row(z + way * hop, lax.rem(base + part, 2))
                    a_ref[pl.ds(start, 16), :] = lefts[which][first + index, a]
            left = solve(a_ref[...], w_ref[...])
            product = lax.dot_general(left, f_ref[b], dims, preferred_element_type=jnp.float32)
            out_ref[slot] = (-product).astype(jnp.bfloat16)

        @pl.when(slot >= live)
        def _():
            out_ref[slot] = jnp.zeros_like(out_ref[slot])


def pairs(*hops):
    return tuple((hop, part) for hop in hops for part in range(2))


def body(panel, inverse_factor, slot_rows, slot_cols, live_count):
    piece = panel[:, 0]
    size = inverse_factor.shape[0]
    core = lax.axis_index("col") % 2

    other = swap_core(piece)
    pair = jnp.stack([piece, other])
    g4 = spread_z(pair, 4)
    mine = jnp.stack(
        [
            lax.dynamic_index_in_dim(part.reshape(2, 2, *piece.shape[1:]), core, 1, keepdims=False)
            for part in (piece, other)
        ]
    )
    scattered, g4 = lax.optimization_barrier((scatter(mine), g4))
    fanned = jnp.broadcast_to(scattered[None], (ROWS, *scattered.shape))
    right = lax.all_to_all(fanned, "row", 0, 0, tiled=True)

    near = jnp.concatenate([pair, g4])
    g3 = spread_z(near, 3)
    g1a = spread_z(near, 1)
    g1b = spread_z(jnp.concatenate([g1a, g3[2:3]]), 1)
    early = jnp.concatenate([g4, g3, g1a])
    lefts = [pair, early, g1b, swap_core(early), swap_core(g1b)]
    hops = pairs(4, 3, 7, 1, 5)
    last = pairs(2, 6) + ((8, 0),)
    plan = (
        (0, 0, pairs(0), False),
        (1, 0, hops, False),
        (2, 0, last, False),
        (3, 0, hops, True),
        (4, 0, last, True),
    )

    smem = pl.BlockSpec(memory_space=pltpu.SMEM)
    vmem = pl.BlockSpec(memory_space=pltpu.VMEM)
    blocks = jax.ShapeDtypeStruct((2, size, size), jnp.bfloat16)
    params = pltpu.CompilerParams(vmem_limit_bytes=8 * 2**20)
    solved = pl.pallas_call(
        right_kernel,
        out_shape=blocks,
        in_specs=[vmem] * 2,
        out_specs=vmem,
        scratch_shapes=[pltpu.VMEM((size, size), jnp.bfloat16)],
        cost_estimate=pl.CostEstimate(flops=4 * size**3, bytes_accessed=2**22, transcendentals=0),
        compiler_params=params,
    )(inverse_factor, right)
    out = pl.pallas_call(
        functools.partial(update_kernel, plan),
        out_shape=blocks,
        in_specs=[smem] * 3 + [vmem] * (2 + len(lefts)),
        out_specs=vmem,
        scratch_shapes=[pltpu.VMEM((size, size), jnp.bfloat16)],
        compiler_params=params,
    )(slot_rows, slot_cols, live_count, inverse_factor, solved, *lefts)
    return out[None, None]


def solution(mesh):
    placed = (
        P(None, "row", "col", None),
        P(),
        P("row", "col", None),
        P("row", "col", None),
        P("row", "col"),
    )
    return jax.shard_map(
        body,
        mesh=mesh,
        in_specs=placed,
        out_specs=P("row", "col", None, None, None),
        check_vma=False,
    )
```
